32 devices in a mesh: tm: 4 (over x, core), chan: 8 (over z, y).
Axes of the slice: x: 2, y: 2, z: 4, core: 2. Of those that a mesh axis runs over, the one named last changes fastest.
Arguments:
- samples: bfloat16 [384, 128], P('chan', 'tm'), may hold values from -6 to 6
- dead_channels: int32 [12], replicated, may hold values from 0 to 383
- first_kernel: bfloat16 [8, 32], replicated, may hold values from -3 to 3
- dilated_one: bfloat16 [3, 32, 64], replicated, may hold values from -0.875 to 0.875
- dilated_two: bfloat16 [3, 64, 128], replicated, may hold values from -0.625 to 0.625
- dilated_three: bfloat16 [3, 128, 256], replicated, may hold values from -0.4375 to 0.4375
- dilated_four: bfloat16 [3, 256, 256], replicated, may hold values from -0.3125 to 0.3125
- embed_weight: bfloat16 [256, 512], replicated, may hold values from -0.375 to 0.375
- gain_one: float32 [512], replicated, may hold values from 0.1 to 1.9
- project_in: bfloat16 [512, 1536], replicated, may hold values from -1 to 1
- project_out: bfloat16 [512, 512], replicated, may hold values from -0.25 to 0.25
- gain_two: float32 [512], replicated, may hold values from 0.1 to 1.9
- up_weight: bfloat16 [512, 2048], replicated, may hold values from -0.25 to 0.25
- down_weight: bfloat16 [2048, 512], replicated, may hold values from -0.125 to 0.125
Outputs:
- encoded: bfloat16 [32, 384, 512], P('tm', 'chan')
The draws below stay inside these ranges and needn't reach their ends.
Inputs may be any that keep to these rules, and one draw needn't show every extreme that they name: `dead_channels`: channel numbers; a number may repeat.
All inputs are finite; a program needn't handle non-finite values.
Results may differ from the reference program's by a relative error of at most 0.015.
Values may be sent and summed in bfloat16 or wider, within the bound.
A program may use at most 64 MiB of HBM per device.

```python
import jax
import jax.numpy as jnp
from jax import lax

D = 512
HEADS = 8
FF = 2048
C1 = 32
C2 = 64
C3 = 128
C4 = 256
KERNEL = 8
STRIDE = 4
NC = 384
F = 32
NS = 128
NDEAD = 12


def draw_project_in(key, part):
    first, second, third = jax.random.split(jax.random.fold_in(key, 11), 3)
    scaling = D ** (-0.5)
    queries = jax.random.normal(first, (D, D), jnp.float32) * scaling
    keys_part = jax.random.normal(second, (D, D), jnp.float32) * scaling
    values_part = jax.random.normal(third, (D, D), jnp.float32) * scaling
    joined = jnp.concatenate([queries, keys_part, values_part], axis=1)
    return jnp.clip(joined, -1.0, 1.0).astype(jnp.bfloat16)


def plant(result, stream_key, low, high):
    index_at = [jax.random.randint(jax.random.fold_in(stream_key, axis), (), 0, length) for axis, length in enumerate(result.shape)]
    widest = result.shape.index(max(result.shape))
    neighbour = index_at[:widest] + [(index_at[widest] + 1) % result.shape[widest]] + index_at[widest + 1:]
    return result.at[tuple(index_at)].set(low).at[tuple(neighbour)].set(high)


def steps_of(stream_key, shape, cuts, smallest, top_value):
    level, own = 1.0, jax.random.fold_in(stream_key, 6)
    for dim, blocks in cuts:
        draws = jnp.exp(jax.random.uniform(jax.random.fold_in(own, dim), (blocks,), jnp.float32, smallest / len(cuts), top_value / len(cuts)))
        level = level * jnp.repeat(draws, shape[dim] // blocks).reshape([-1 if axis == dim else 1 for axis in range(len(shape))])
    return level


def noise(stream_key, dims, deviation, limit, cuts=(), kind=jnp.bfloat16):
    entries = jax.random.normal(stream_key, dims, jnp.float32) * deviation
    if len(cuts) > 0:
        entries = steps_of(stream_key, dims, cuts, -0.22, 0.18) * entries
    return jnp.clip(entries, min=-limit, max=limit).astype(kind)


def setup_inputs(seed: int = 0) -> dict:
    streams_of = jax.random.split(jax.random.key(seed), 15)
    return {
        "samples": noise(streams_of[0], (NC, NS), 1.0, 6.0, ((0, 8), (1, 4))),
        "dead_channels": plant(jax.random.randint(streams_of[1], (NDEAD,), 0, NC), jax.random.fold_in(streams_of[1], 1), 0, NC - 1).astype(jnp.int32),
        "first_kernel": noise(streams_of[2], (KERNEL, C1), (KERNEL // 2) ** -0.5, 3.0),
        "dilated_one": noise(streams_of[3], (3, C1, C2), (3 * C1 // 2) ** -0.5, 0.875),
        "dilated_two": noise(streams_of[4], (3, C2, C3), (3 * C2 // 2) ** -0.5, 0.625),
        "dilated_three": noise(streams_of[5], (3, C3, C4), (3 * C3 // 2) ** -0.5, 0.4375),
        "dilated_four": noise(streams_of[6], (3, C4, C4), (3 * C4 // 2) ** -0.5, 0.3125),
        "embed_weight": noise(streams_of[7], (C4, D), C4 ** -0.5, 0.375),
        "gain_one": jnp.clip(1.0 + 0.18 * jax.random.normal(streams_of[8], (D,), jnp.float32), 0.1, 1.9),
        "project_in": draw_project_in(jax.random.fold_in(streams_of[14], 71), 0),
        "project_out": noise(streams_of[10], (D, D), D ** -0.5, 0.25),
        "gain_two": jnp.clip(1.0 + 0.18 * jax.random.normal(streams_of[11], (D,), jnp.float32), 0.1, 1.9),
        "up_weight": noise(streams_of[12], (D, FF), D ** -0.5, 0.25),
        "down_weight": noise(streams_of[13], (FF, D), FF ** -0.5, 0.125),
    }


EPSILON = 1e-05
DILATIONS = (1, 2, 4, 8)

def normalize(tokens, gain):
    floats = tokens.astype(jnp.float32)
    average = lax.optimization_barrier(jnp.mean(floats, axis=-1, keepdims=True))
    centred = floats - average
    variance = lax.optimization_barrier(jnp.mean(centred * centred, axis=-1, keepdims=True))
    return (centred * lax.rsqrt(variance + EPSILON) * gain.astype(jnp.float32)).astype(jnp.bfloat16)

def attend(query_rows, key_rows, value_rows, alive_mask):
    count = query_rows.shape[0]
    block_rows = min(512, count)
    scaling = query_rows.shape[2] ** (-0.5)

    def one_head(operands):
        queries, keys_head, values_head = operands
        blocks = queries.reshape(count // block_rows, block_rows, queries.shape[1])

        def one_block(query_block):
            scores = jnp.dot(query_block, keys_head.T, preferred_element_type=jnp.float32) * scaling
            scores = jnp.where(alive_mask[None, :], scores, -1e+30)
            largest = lax.optimization_barrier(jnp.max(scores, axis=1, keepdims=True))
            exponent = jnp.exp(scores - largest)
            weights = (exponent / lax.optimization_barrier(jnp.sum(exponent, axis=1, keepdims=True))).astype(jnp.bfloat16)
            return jnp.dot(weights, values_head, preferred_element_type=jnp.float32).astype(jnp.bfloat16)
        return lax.map(one_block, blocks).reshape(count, queries.shape[1])
    heads_first = lax.map(one_head, (jnp.swapaxes(query_rows, 0, 1), jnp.swapaxes(key_rows, 0, 1), jnp.swapaxes(value_rows, 0, 1)))
    return jnp.swapaxes(heads_first, 0, 1).reshape(count, -1)

def encoder(embedded, alive_mask, gain_one, project_in, project_out, gain_two, up_weight, down_weight):
    count, width = embedded.shape
    normed = normalize(embedded, gain_one)
    projected = jnp.dot(normed, project_in, preferred_element_type=jnp.float32).astype(jnp.bfloat16)
    pieces = projected.reshape(count, 3, HEADS, width // HEADS)
    attended = attend(pieces[:, 0], pieces[:, 1], pieces[:, 2], alive_mask)
    mixed = (embedded.astype(jnp.float32) + jnp.dot(attended, project_out, preferred_element_type=jnp.float32)).astype(jnp.bfloat16)
    normed_two = normalize(mixed, gain_two)
    inner = jax.nn.gelu(jnp.dot(normed_two, up_weight, preferred_element_type=jnp.float32)).astype(jnp.bfloat16)
    return (mixed.astype(jnp.float32) + jnp.dot(inner, down_weight, preferred_element_type=jnp.float32)).astype(jnp.bfloat16)

def patch_conv(padded, first_kernel, frames):
    taps = jnp.stack([padded[:, offset:offset + STRIDE * (frames - 1) + 1:STRIDE] for offset in range(KERNEL)], axis=-1)
    summed = jnp.einsum('cfk,ko->fco', taps.astype(jnp.float32), first_kernel.astype(jnp.float32))
    return jax.nn.gelu(summed).astype(jnp.bfloat16)

def dilated(padded, weight, dilation, frames):
    summed = jnp.zeros((frames, padded.shape[1], weight.shape[2]), jnp.float32)
    for offset in range(3):
        window = padded[offset * dilation:offset * dilation + frames]
        summed = summed + jnp.einsum('fci,io->fco', window.astype(jnp.float32), weight[offset].astype(jnp.float32))
    return jax.nn.gelu(summed).astype(jnp.bfloat16)

def reference(samples, dead_channels, first_kernel, dilated_one, dilated_two, dilated_three, dilated_four, embed_weight, gain_one, project_in, project_out, gain_two, up_weight, down_weight):
    channel_ids = jnp.arange(NC, dtype=jnp.int32)
    alive_mask = jnp.logical_not(jnp.any(channel_ids[:, None] == dead_channels[None, :], axis=1))
    signal = jnp.where(alive_mask[:, None], samples, jnp.zeros_like(samples))
    rim_width = (KERNEL - STRIDE) // 2
    padded = jnp.pad(signal, ((0, 0), (rim_width, rim_width)))
    hidden = patch_conv(padded, first_kernel, F)
    for weight, dilation in zip((dilated_one, dilated_two, dilated_three, dilated_four), DILATIONS):
        extended = jnp.pad(hidden, ((dilation, dilation), (0, 0), (0, 0)))
        hidden = dilated(extended, weight, dilation, F)
    embedded = jnp.einsum('fci,io->fco', hidden.astype(jnp.float32), embed_weight.astype(jnp.float32)).astype(jnp.bfloat16)

    def per_frame(frame_tokens):
        return encoder(frame_tokens, alive_mask, gain_one, project_in, project_out, gain_two, up_weight, down_weight)
    return lax.map(per_frame, embedded)
```

```python
import functools

import jax
import jax.numpy as jnp
from jax import lax
from jax.experimental import pallas as pl
from jax.experimental.pallas import tpu as pltpu
from jax.sharding import PartitionSpec as P

HEADS = 8
STRIDE = 4
EPSILON = 1e-05
REACH = 15
CONV_ROWS = 384
QUERY_ROWS = 192
STACK = 4
MESH = pl.DeviceIdType.MESH


def gelu(v):
    half = 0.5 * v
    return half + half * jnp.tanh(v * (0.7978845608028654 + 0.035677408136300125 * (v * v)))


def dot(a, b):
    return jnp.dot(a, b, preferred_element_type=jnp.float32)


def normalize(tokens, gain):
    floats = tokens.astype(jnp.float32)
    centred = floats - jnp.mean(floats, axis=-1, keepdims=True)
    variance = jnp.mean(centred * centred, axis=-1, keepdims=True)
    return (centred * lax.rsqrt(variance + EPSILON) * gain).astype(jnp.bfloat16)


def looped(count, body):
    if count == 1:
        body(0)
    else:
        lax.fori_loop(0, count, lambda i, c: (body(i), c)[1], 0)


def kernel(
    groups_t,
    groups_c,
    dead_hbm,
    samples_hbm,
    first_hbm,
    one_hbm,
    two_hbm,
    three_hbm,
    four_hbm,
    embed_hbm,
    gain_one_hbm,
    pin_hbm,
    pout_hbm,
    gain_two_hbm,
    up_hbm,
    down_hbm,
    out,
    gathered,
    signal,
    toeplitz,
    one_wide,
    h0,
    h1,
    h2,
    h3,
    embedded,
    qkv,
    attended,
    result,
    dead,
    samples,
    first_kernel,
    one,
    gain_one,
    gain_two,
    two,
    three,
    four,
    embed,
    pin,
    pout,
    up,
    down,
    weight_sem,
    send_sem,
    recv_sem,
    hand_send,
    hand_recv,
    out_send,
    out_recv,
    own_sem,
):
    my_t, my_c = lax.axis_index("tm"), lax.axis_index("chan")
    me = my_t * groups_c + my_c
    slab, held = samples.shape
    pack_rows = gathered.shape[1]
    packs = held // pack_rows
    total_samples = groups_t * slab
    frames = total_samples // STRIDE
    tokens = groups_c * held
    frame = my_t * (slab // STRIDE) + my_c

    barrier = pltpu.get_barrier_semaphore()

    def greet_chan(i):
        peer = lax.rem(my_c + 1 + i, groups_c)
        pl.semaphore_signal(barrier, inc=1, device_id=(my_t, peer), device_id_type=MESH)

    def greet_time(i):
        peer = lax.rem(my_t + 1 + i, groups_t)
        pl.semaphore_signal(barrier, inc=1, device_id=(peer, my_c), device_id_type=MESH)

    looped(groups_c - 1, greet_chan)
    looped(groups_t - 1, greet_time)

    loads = [
        pltpu.make_async_copy(src, dst, weight_sem.at[i])
        for i, (src, dst) in enumerate(
            [
                (dead_hbm, dead),
                (samples_hbm, samples),
                (first_hbm, first_kernel),
                (one_hbm, one),
                (gain_one_hbm, gain_one),
                (gain_two_hbm, gain_two),
                (two_hbm, two),
                (three_hbm, three),
                (four_hbm, four),
                (embed_hbm, embed),
                (pin_hbm, pin),
                (pout_hbm, pout),
                (up_hbm, up),
                (down_hbm, down),
            ]
        )
    ]
    for load in loads:
        load.start()
    for load in loads[:4]:
        load.wait()

    row_ids = lax.broadcasted_iota(jnp.int32, (held, held), 0)
    alive = row_ids == lax.broadcasted_iota(jnp.int32, (held, held), 1)
    row_ids = row_ids + my_c * held
    for i in range(dead.shape[0]):
        alive = jnp.logical_and(alive, row_ids != dead[i])
    own = lax.dot_general(
        jnp.where(alive, 1.0, 0.0).astype(jnp.bfloat16),
        samples[...],
        (((1,), (1,)), ((), ())),
        preferred_element_type=jnp.float32,
    ).astype(jnp.bfloat16)
    for a in range(packs):
        gathered[me, :, a * slab : (a + 1) * slab] = own[a * pack_rows : (a + 1) * pack_rows, :]

    pl.semaphore_wait(barrier, groups_c + groups_t - 2)

    def spread(peer, slot):
        return pltpu.make_async_remote_copy(
            src_ref=gathered.at[my_t * groups_c + slot],
            dst_ref=gathered.at[my_t * groups_c + slot],
            send_sem=send_sem.at[peer],
            recv_sem=recv_sem.at[slot],
            device_id=(my_t, peer),
            device_id_type=MESH,
        )

    def hand(peer, slab_at):
        slots = pl.ds(slab_at * groups_c, groups_c)
        return pltpu.make_async_remote_copy(
            src_ref=gathered.at[slots],
            dst_ref=gathered.at[slots],
            send_sem=hand_send.at[peer],
            recv_sem=hand_recv.at[slab_at],
            device_id=(peer, my_c),
            device_id_type=MESH,
        )

    def chan_peer(i):
        return lax.rem(my_c + 1 + i, groups_c)

    def time_peer(i):
        return lax.rem(my_t + 1 + i, groups_t)

    looped(groups_c - 1, lambda i: spread(chan_peer(i), my_c).start())

    c1 = first_kernel.shape[1]
    width = (2 * REACH + 2) * c1
    pick = lax.broadcasted_iota(jnp.int32, (c1, width), 0) == lax.rem(
        lax.broadcasted_iota(jnp.int32, (c1, width), 1), c1
    )
    tiled = dot(first_kernel[...], pick.astype(jnp.float32).astype(jnp.bfloat16))
    c2 = one.shape[1]
    one_wide[...] = jnp.zeros_like(one_wide)
    one_wide[: 3 * c1, :c2] = one[...]
    one_wide[2 * c1 : 5 * c1, c2:] = one[...]

    key_ids = lax.broadcasted_iota(jnp.int32, (1, tokens), 1)
    dead_keys = key_ids < 0
    for i in range(dead.shape[0]):
        dead_keys = jnp.logical_or(dead_keys, key_ids == dead[i])
    key_bias = jnp.where(dead_keys, -1e30, 0.0)

    looped(groups_c - 1, lambda i: spread(chan_peer(i), chan_peer(i)).wait_recv())
    looped(groups_t - 1, lambda i: hand(time_peer(i), my_t).start())

    for start in range(0, total_samples, 128):
        size = min(128, total_samples - start)
        at_sample = lax.broadcasted_iota(jnp.int32, (size, width), 0) + start
        at_frame = lax.broadcasted_iota(jnp.int32, (size, width), 1) // c1 + (frame - REACH)
        tap = at_sample - STRIDE * at_frame + (first_kernel.shape[0] - STRIDE) // 2
        tap = jnp.where(jnp.logical_and(at_frame >= 0, at_frame < frames), tap, -1)
        band = jnp.zeros((size, width), jnp.float32)
        for k in range(first_kernel.shape[0]):
            band = jnp.where(tap == k, tiled[k : k + 1, :], band)
        toeplitz[start : start + size, :] = band.astype(jnp.bfloat16)

    looped(groups_t - 1, lambda i: hand(time_peer(i), time_peer(i)).wait_recv())

    for t in range(groups_t):
        for a in range(packs):
            signal[:, a * pack_rows : (a + 1) * pack_rows, t * slab : (t + 1) * slab] = gathered[
                t * groups_c : (t + 1) * groups_c, :, a * slab : (a + 1) * slab
            ]

    def inside(offset):
        at = frame + offset
        return jnp.logical_and(at >= 0, at < frames).astype(jnp.float32)

    for load in loads[4:11]:
        load.wait()

    def convolve(block):
        chans = CONV_ROWS // held
        rows = pl.ds(pl.multiple_of(block * CONV_ROWS, CONV_ROWS), CONV_ROWS)
        waves = signal[pl.ds(block * chans, chans)].reshape(CONV_ROWS, total_samples)
        for q in range(width // 256):
            cols = slice(q * 256, (q + 1) * 256)
            h0[:, cols] = gelu(dot(waves, toeplitz[:, cols])).astype(jnp.bfloat16)
        later = lax.broadcasted_iota(jnp.int32, (1, 2 * c2), 1) >= c2
        for q in range(8):
            depth = min(5 * c1, width - 128 * q)
            summed = gelu(dot(h0[:, 128 * q : 128 * q + depth], one_wide[:depth, :]))
            keep = jnp.where(later, inside(4 * q + 2 - 14), inside(4 * q - 14))
            h1[:, 128 * q : 128 * (q + 1)] = (summed * keep).astype(jnp.bfloat16)
        for n in range(7):
            summed = gelu(dot(h1[:, 128 * n : 128 * n + 192], two[...]))
            h2[:, 128 * n : 128 * (n + 1)] = (summed * inside(4 * n - 12)).astype(jnp.bfloat16)
        for p in range(3):
            summed = gelu(dot(h2[:, 256 * p : 256 * p + 384], three[...]))
            h3[:, 256 * p : 256 * (p + 1)] = (summed * inside(8 * p - 8)).astype(jnp.bfloat16)
        features = gelu(dot(h3[...], four[...])).astype(jnp.bfloat16)
        embedded_rows = dot(features, embed[...]).astype(jnp.bfloat16)
        embedded[rows, :] = embedded_rows
        normed = normalize(embedded_rows, gain_one[...])
        for q in range(pin.shape[1] // 256):
            cols = slice(q * 256, (q + 1) * 256)
            qkv[rows, cols] = dot(normed, pin[:, cols]).astype(jnp.bfloat16)

    looped(tokens // CONV_ROWS, convolve)

    for load in loads[11:]:
        load.wait()

    model = embed.shape[1]
    head = model // HEADS
    blocks = tokens // QUERY_ROWS
    peers = QUERY_ROWS // held
    my_block = my_c // peers

    def back(peer):
        return pltpu.make_async_remote_copy(
            src_ref=result.at[peer],
            dst_ref=out.at[my_c],
            send_sem=out_send.at[peer],
            recv_sem=out_recv.at[my_c],
            device_id=(my_t, peer),
            device_id_type=MESH,
        )

    keep_own = pltpu.make_async_copy(result.at[my_c], out.at[my_c], own_sem)

    def encode(step):
        half = blocks // 2
        far = 1 - step // half
        side = lax.rem(my_block // half + far, 2)
        block = side * half + lax.rem(my_block + 1 + step, half)
        rows = pl.ds(pl.multiple_of(block * QUERY_ROWS, QUERY_ROWS), QUERY_ROWS)
        span = STACK * head
        lane_head = lax.broadcasted_iota(jnp.int32, (1, span), 1) // head
        for base in range(0, model, span):
            queries = qkv[rows, base : base + span].astype(jnp.float32) * (head**-0.5)
            keys = qkv[:, model + base : model + base + span]
            values = qkv[:, 2 * model + base : 2 * model + base + span]
            stacked = jnp.concatenate(
                [jnp.where(lane_head == h, queries, 0.0).astype(jnp.bfloat16) for h in range(STACK)], axis=0
            )
            scores = lax.dot_general(
                stacked, keys, (((1,), (1,)), ((), ())), preferred_element_type=jnp.float32
            )
            scores = scores + key_bias
            exponent = jnp.exp(scores - jnp.max(scores, axis=1, keepdims=True))
            total = jnp.sum(exponent, axis=1, keepdims=True)
            mean = dot(exponent.astype(jnp.bfloat16), values) / total
            merged = mean[:QUERY_ROWS]
            for h in range(1, STACK):
                merged = jnp.where(lane_head == h, mean[h * QUERY_ROWS : (h + 1) * QUERY_ROWS], merged)
            attended[:, base : base + span] = merged.astype(jnp.bfloat16)
        mixed = (embedded[rows, :].astype(jnp.float32) + dot(attended[...], pout[...])).astype(jnp.bfloat16)
        normed = normalize(mixed, gain_two[...])
        total = mixed.astype(jnp.float32)
        for q in range(up.shape[1] // 512):
            cols = slice(q * 512, (q + 1) * 512)
            inner = gelu(dot(normed, up[:, cols])).astype(jnp.bfloat16)
            total = total + dot(inner, down[cols, :])
        result[pl.ds(block * peers, peers)] = total.astype(jnp.bfloat16).reshape(peers, held, model)
        for i in range(peers):
            peer = block * peers + i

            @pl.when(peer != my_c)
            def _():
                back(peer).start()

            @pl.when(peer == my_c)
            def _():
                keep_own.start()

    looped(blocks, encode)

    looped(groups_c - 1, lambda i: spread(chan_peer(i), my_c).wait_send())
    looped(groups_t - 1, lambda i: hand(time_peer(i), my_t).wait_send())

    def finish(i):
        peer = lax.rem(my_c + 1 + i, groups_c)
        back(peer).wait_send()
        pltpu.make_async_remote_copy(
            src_ref=result.at[peer],
            dst_ref=out.at[peer],
            send_sem=out_send.at[peer],
            recv_sem=out_recv.at[peer],
            device_id=(my_t, peer),
            device_id_type=MESH,
        ).wait_recv()

    looped(groups_c - 1, finish)
    keep_own.wait()


def per_device(
    samples,
    dead_channels,
    first_kernel,
    dilated_one,
    dilated_two,
    dilated_three,
    dilated_four,
    embed_weight,
    gain_one,
    project_in,
    project_out,
    gain_two,
    up_weight,
    down_weight,
):
    groups_t, groups_c = lax.axis_size("tm"), lax.axis_size("chan")
    held, slab = samples.shape
    assert slab // STRIDE == groups_c
    devices = groups_t * groups_c
    tokens = groups_c * held
    packs = 3 if slab * 3 <= 128 and held % 48 == 0 else 1
    model = embed_weight.shape[1]
    flat = [w.reshape(w.shape[0] * w.shape[1], w.shape[2]) for w in (dilated_one, dilated_two, dilated_three, dilated_four)]
    bf16 = jnp.bfloat16
    width = (2 * REACH + 2) * first_kernel.shape[1]
    anywhere = pl.BlockSpec(memory_space=pl.ANY)
    like = lambda w: pltpu.VMEM(w.shape, w.dtype)
    return pl.pallas_call(
        functools.partial(kernel, groups_t, groups_c),
        out_shape=pltpu.VMEM((groups_c, held, model), bf16),
        in_specs=[anywhere] * 14,
        out_specs=anywhere,
        scratch_shapes=[
            pltpu.VMEM((devices, held // packs, 128 if packs > 1 else slab), bf16),
            pltpu.VMEM((groups_c, held, groups_t * slab), bf16),
            pltpu.VMEM((groups_t * slab, width), bf16),
            pltpu.VMEM((5 * dilated_one.shape[1], 2 * dilated_one.shape[2]), bf16),
            pltpu.VMEM((CONV_ROWS, width), bf16),
            pltpu.VMEM((CONV_ROWS, 8 * 128), bf16),
            pltpu.VMEM((CONV_ROWS, 7 * 128), bf16),
            pltpu.VMEM((CONV_ROWS, 3 * 256), bf16),
            pltpu.VMEM((tokens, model), bf16),
            pltpu.VMEM((tokens, 3 * model), bf16),
            pltpu.VMEM((QUERY_ROWS, model), bf16),
            pltpu.VMEM((groups_c, held, model), bf16),
            pltpu.SMEM(dead_channels.shape, dead_channels.dtype),
            pltpu.VMEM((slab, held), bf16),
            like(first_kernel),
            like(flat[0]),
            pltpu.VMEM((1, model), jnp.float32),
            pltpu.VMEM((1, model), jnp.float32),
        ]
        + [like(w) for w in flat[1:]]
        + [like(w) for w in (embed_weight, project_in, project_out, up_weight, down_weight)]
        + [
            pltpu.SemaphoreType.DMA((14,)),
            pltpu.SemaphoreType.DMA((groups_c,)),
            pltpu.SemaphoreType.DMA((groups_c,)),
            pltpu.SemaphoreType.DMA((groups_t,)),
            pltpu.SemaphoreType.DMA((groups_t,)),
            pltpu.SemaphoreType.DMA((groups_c,)),
            pltpu.SemaphoreType.DMA((groups_c,)),
            pltpu.SemaphoreType.DMA,
        ],
        compiler_params=pltpu.CompilerParams(
            collective_id=0, has_side_effects=True, vmem_limit_bytes=44 * 2**20
        ),
    )(
        *[
            pltpu.with_memory_space_constraint(w, pltpu.HBM)
            for w in (
                dead_channels,
                samples.T,
                first_kernel,
                *flat,
                embed_weight,
                gain_one.reshape(1, -1),
                project_in,
                project_out,
                gain_two.reshape(1, -1),
                up_weight,
                down_weight,
            )
        ]
    )


def solution(mesh):
    return jax.shard_map(
        per_device,
        mesh=mesh,
        in_specs=(P("chan", "tm"), P(), P(), P(), P(), P(), P(), P(), P(), P(), P(), P(), P(), P()),
        out_specs=P("tm", "chan", None),
        check_vma=False,
    )
```

```python
import functools

import jax
import jax.numpy as jnp
from jax import lax
from jax.experimental import pallas as pl
from jax.experimental.pallas import tpu as pltpu
from jax.sharding import PartitionSpec as P

HEADS = 8
STRIDE = 4
EPSILON = 1e-05
REACH = 15
APART = 4
SPAN = 2 * REACH + APART + 2
ROWS = 192
MESH = pl.DeviceIdType.MESH
BF16 = jnp.bfloat16


def gelu(v, half=0.5):
    v = v.astype(BF16)
    scaled = v * jnp.asarray(half, BF16)
    return scaled + scaled * jnp.tanh(v * (BF16(0.7978845608028654) + BF16(0.035677408136300125) * (v * v)))


def dot(a, b):
    return jnp.dot(a, b, preferred_element_type=jnp.float32)


def dot_nt(a, b):
    return lax.dot_general(a, b, (((1,), (1,)), ((), ())), preferred_element_type=jnp.float32)


def normalize(tokens, gain):
    floats = tokens.astype(jnp.float32)
    centred = floats - jnp.mean(floats, axis=-1, keepdims=True)
    variance = jnp.mean(centred * centred, axis=-1, keepdims=True)
    return (centred * lax.rsqrt(variance + EPSILON) * gain).astype(BF16)


def looped(count, body):
    if count == 1:
        body(0)
    else:
        lax.fori_loop(0, count, lambda i, c: (body(i), c)[1], 0)


def kernel(
    groups_t,
    groups_c,
    dead_hbm,
    samples_hbm,
    first_hbm,
    one_hbm,
    two_hbm,
    three_hbm,
    four_hbm,
    embed_hbm,
    gain_one_hbm,
    pin_hbm,
    pout_hbm,
    gain_two_hbm,
    up_hbm,
    down_hbm,
    out,
    raw,
    signal,
    toeplitz,
    one_wide,
    key_bias,
    h0,
    h1,
    h2,
    h3,
    embedded,
    queries,
    keys,
    values,
    attended,
    inner,
    result,
    dead,
    first_kernel,
    one,
    gain_one,
    gain_two,
    two,
    three,
    four,
    embed,
    pin,
    pout,
    up,
    down,
    weight_sem,
    send_sem,
    recv_sem,
    hand_send,
    hand_recv,
    out_send,
    out_recv,
    own_sem,
):
    my_t, my_c = lax.axis_index("tm"), lax.axis_index("chan")
    slab, held = raw.shape[1:]
    total_samples = groups_t * slab
    frames = total_samples // STRIDE
    tokens = groups_c * held
    mates = groups_c // 2
    my_half, my_place = lax.div(my_c, mates), lax.rem(my_c, mates)

    def slot_of(place):
        return lax.div(place, APART) * (2 * APART) + lax.rem(place, APART)

    frame = my_t * (slab // STRIDE) + slot_of(my_place)

    barrier = pltpu.get_barrier_semaphore()

    def chan_peer(i):
        return lax.rem(my_c + 1 + i, groups_c)

    def time_peer(i):
        return lax.rem(my_t + 1 + i, groups_t)

    def greet_chan(i):
        pl.semaphore_signal(barrier, inc=1, device_id=(my_t, chan_peer(i)), device_id_type=MESH)

    def greet_time(i):
        pl.semaphore_signal(barrier, inc=1, device_id=(time_peer(i), my_c), device_id_type=MESH)

    looped(groups_c - 1, greet_chan)
    looped(groups_t - 1, greet_time)

    loads = [
        pltpu.make_async_copy(src, dst, weight_sem.at[i])
        for i, (src, dst) in enumerate(
            [
                (dead_hbm, dead),
                (samples_hbm, raw.at[my_t]),
                (first_hbm, first_kernel),
                (one_hbm, one),
                (gain_one_hbm, gain_one),
                (gain_two_hbm, gain_two),
                (two_hbm, two),
                (three_hbm, three),
                (four_hbm, four),
                (embed_hbm, embed),
                (pin_hbm, pin),
                (pout_hbm, pout),
                (up_hbm, up),
                (down_hbm, down),
            ]
        )
    ]
    for load in loads:
        load.start()

    pl.semaphore_wait(barrier, groups_c + groups_t - 2)

    def hand(peer, slab_at):
        return pltpu.make_async_remote_copy(
            src_ref=samples_hbm,
            dst_ref=raw.at[slab_at],
            send_sem=hand_send.at[peer],
            recv_sem=hand_recv.at[slab_at],
            device_id=(peer, my_c),
            device_id_type=MESH,
        )

    def spread(peer, slot):
        return pltpu.make_async_remote_copy(
            src_ref=signal.at[slot],
            dst_ref=signal.at[slot],
            send_sem=send_sem.at[peer],
            recv_sem=recv_sem.at[slot],
            device_id=(my_t, peer),
            device_id_type=MESH,
        )

    looped(groups_t - 1, lambda i: hand(time_peer(i), my_t).start())

    for load in loads[:4]:
        load.wait()

    row_ids = lax.broadcasted_iota(jnp.int32, (held, held), 0)
    alive = row_ids == lax.broadcasted_iota(jnp.int32, (held, held), 1)
    row_ids = row_ids + my_c * held
    for i in range(dead.shape[0]):
        alive = jnp.logical_and(alive, row_ids != dead[i])
    alive = jnp.where(alive, 1.0, 0.0).astype(BF16)

    looped(groups_t - 1, lambda i: hand(time_peer(i), time_peer(i)).wait_recv())

    own = dot_nt(alive, raw[...].reshape(total_samples, held))
    signal[my_c] = own.astype(BF16)
    looped(groups_c - 1, lambda i: spread(chan_peer(i), my_c).start())

    c1 = first_kernel.shape[1]
    width = SPAN * c1
    pick = lax.broadcasted_iota(jnp.int32, (c1, width), 0) == lax.rem(
        lax.broadcasted_iota(jnp.int32, (c1, width), 1), c1
    )
    tiled = dot(first_kernel[...], pick.astype(jnp.float32).astype(BF16))
    c2 = one.shape[1]
    one_wide[...] = jnp.zeros_like(one_wide)
    one_wide[: 3 * c1, :c2] = one[...]
    one_wide[2 * c1 : 5 * c1, c2:] = one[...]

    for start in range(0, tokens, 384):
        shape = (384, 128)
        key_ids = lax.broadcasted_iota(jnp.int32, shape, 0) + start
        dead_keys = key_ids < 0
        for i in range(dead.shape[0]):
            dead_keys = jnp.logical_or(dead_keys, key_ids == dead[i])
        dead_keys = jnp.logical_and(dead_keys, lax.broadcasted_iota(jnp.int32, shape, 1) == 0)
        key_bias[start : start + 384, :] = jnp.where(dead_keys, -1e30, 0.0).astype(BF16)

    for start in range(0, total_samples, 128):
        size = min(128, total_samples - start)
        at_sample = lax.broadcasted_iota(jnp.int32, (size, width), 0) + start
        at_frame = lax.broadcasted_iota(jnp.int32, (size, width), 1) // c1 + (frame - REACH)
        tap = at_sample - STRIDE * at_frame + (first_kernel.shape[0] - STRIDE) // 2
        tap = jnp.where(jnp.logical_and(at_frame >= 0, at_frame < frames), tap, -1)
        band = jnp.zeros((size, width), jnp.float32)
        for k in range(first_kernel.shape[0]):
            band = jnp.where(tap == k, tiled[k : k + 1, :], band)
        toeplitz[start : start + size, :] = band.astype(BF16)

    def half_inside(offset):
        at = frame + offset
        return jnp.where(jnp.logical_and(at >= 0, at < frames), 0.5, 0.0)

    def flat_half(offset, lanes):
        return jnp.full((1, lanes), half_inside(offset), jnp.float32).astype(BF16)

    for load in loads[4:11]:
        load.wait()

    model = embed.shape[1]
    head = model // HEADS
    chans = ROWS // held
    half_blocks = mates // chans

    def convolve(mine, step):
        block = step + half_blocks * (my_half if mine else 1 - my_half)
        for i in range(chans):
            peer = block * chans + i

            @pl.when(peer != my_c)
            def _():
                spread(peer, peer).wait_recv()

        waves = signal[pl.ds(block * chans, chans)].reshape(ROWS, total_samples)
        for q in range(width // 384):
            cols = slice(q * 384, (q + 1) * 384)
            h0[:, cols] = gelu(dot(waves, toeplitz[:, cols]))
        later = lax.broadcasted_iota(jnp.int32, (1, 2 * c2), 1) >= c2
        for q in range(9):
            depth = min(5 * c1, width - 128 * q)
            keep = jnp.where(later, half_inside(4 * q + 2 - 14), half_inside(4 * q - 14)).astype(BF16)
            h1[:, 128 * q : 128 * (q + 1)] = gelu(dot(h0[:, 128 * q : 128 * q + depth], one_wide[:depth, :]), keep)
        for n in range(8):
            h2[:, 128 * n : 128 * (n + 1)] = gelu(
                dot(h1[:, 128 * n : 128 * n + 192], two[...]), flat_half(4 * n - 12, 128)
            )
        for k in range(2):
            for p in range(3):
                at = 256 * p + 128 * k
                h3[k * ROWS : (k + 1) * ROWS, 256 * p : 256 * (p + 1)] = gelu(
                    dot(h2[:, at : at + 384], three[...]), flat_half(APART * k + 8 * p - 8, 256)
                )
        features = gelu(dot(h3[...], four[...]))
        embedded_rows = dot(features, embed[...]).astype(BF16)
        normed = normalize(embedded_rows, gain_one[...])
        rows = pl.ds(pl.multiple_of(block * ROWS, ROWS), ROWS)
        for q in range(model // 256):
            cols = slice(q * 256, (q + 1) * 256)
            part = dot(normed, pin[:, model + q * 256 : model + (q + 1) * 256]).astype(BF16)
            keys[0, rows, cols] = part[:ROWS]
            keys[1, rows, cols] = part[ROWS:]
            part = dot(normed, pin[:, 2 * model + q * 256 : 2 * model + (q + 1) * 256]).astype(BF16)
            values[0, rows, cols] = part[:ROWS]
            values[1, rows, cols] = part[ROWS:]
        if mine:
            own_rows = pl.ds(pl.multiple_of(step * ROWS, ROWS), ROWS)
            embedded[0, own_rows, :] = embedded_rows[:ROWS]
            embedded[1, own_rows, :] = embedded_rows[ROWS:]
            for q in range(model // 256):
                cols = slice(q * 256, (q + 1) * 256)
                part = (dot(normed, pin[:, cols]).astype(BF16).astype(jnp.float32) * (head**-0.5)).astype(BF16)
                queries[0, own_rows, cols] = part[:ROWS]
                queries[1, own_rows, cols] = part[ROWS:]

    looped(half_blocks, functools.partial(convolve, True))
    looped(half_blocks, functools.partial(convolve, False))

    for load in loads[11:]:
        load.wait()

    def back(k, place):
        return pltpu.make_async_remote_copy(
            src_ref=result.at[k, place],
            dst_ref=out.at[slot_of(my_place) + APART * k],
            send_sem=out_send.at[k, place],
            recv_sem=out_recv.at[slot_of(my_place) + APART * k],
            device_id=(my_t, my_half * mates + place),
            device_id_type=MESH,
        )

    def keep_own(k):
        return pltpu.make_async_copy(
            result.at[k, my_place], out.at[slot_of(my_place) + APART * k], own_sem.at[k]
        )

    def encode(k, step):
        rows = pl.ds(pl.multiple_of(step * ROWS, ROWS), ROWS)
        first_head = lax.broadcasted_iota(jnp.int32, (1, 2 * head), 1) < head
        unit = (lax.broadcasted_iota(jnp.int32, (2 * ROWS, 128), 1) == 0).astype(jnp.float32).astype(BF16)
        ones = jnp.ones((tokens, 128), BF16)
        nothing = jnp.zeros((ROWS, 2 * head), BF16)
        for base in range(0, model, 2 * head):
            cols = slice(base, base + 2 * head)
            pair = queries[k, rows, cols]
            stacked = jnp.concatenate(
                [jnp.where(first_head, pair, nothing), jnp.where(first_head, nothing, pair)], axis=0
            )
            scores = dot_nt(
                jnp.concatenate([stacked, unit], axis=1), jnp.concatenate([keys[k, :, cols], key_bias[...]], axis=1)
            )
            exponent = jnp.exp((scores - jnp.max(scores, axis=1, keepdims=True)).astype(BF16))
            mean = dot(exponent, jnp.concatenate([values[k, :, cols], ones], axis=1))
            summed = jnp.where(first_head, mean[:ROWS, :128], mean[ROWS:, :128])
            total = jnp.where(first_head, mean[:ROWS, 128:], mean[ROWS:, 128:])
            attended[:, cols] = (summed / total).astype(BF16)
        mixed = (embedded[k, rows, :].astype(jnp.float32) + dot(attended[...], pout[...])).astype(BF16)
        normed = normalize(mixed, gain_two[...])
        for q in range(up.shape[1] // 512):
            cols = slice(q * 512, (q + 1) * 512)
            inner[:, cols] = gelu(dot(normed, up[:, cols]))
        total = mixed.astype(jnp.float32) + dot(inner[...], down[...])
        result[k, pl.ds(step * chans, chans)] = total.astype(BF16).reshape(chans, held, model)

    for k in range(2):
        looped(half_blocks, functools.partial(encode, k))
        looped(mates - 1, lambda i: back(k, lax.rem(my_place + 1 + i, mates)).start())
        keep_own(k).start()

    looped(groups_t - 1, lambda i: hand(time_peer(i), my_t).wait_send())
    looped(groups_c - 1, lambda i: spread(chan_peer(i), my_c).wait_send())

    for k in range(2):

        def finish(i):
            place = lax.rem(my_place + 1 + i, mates)
            back(k, place).wait_send()
            at = slot_of(place) + APART * k
            pltpu.make_async_remote_copy(
                src_ref=result.at[k, place],
                dst_ref=out.at[at],
                send_sem=out_send.at[k, place],
                recv_sem=out_recv.at[at],
                device_id=(my_t, my_half * mates + place),
                device_id_type=MESH,
            ).wait_recv()

        looped(mates - 1, finish)
        keep_own(k).wait()


def per_device(
    samples,
    dead_channels,
    first_kernel,
    dilated_one,
    dilated_two,
    dilated_three,
    dilated_four,
    embed_weight,
    gain_one,
    project_in,
    project_out,
    gain_two,
    up_weight,
    down_weight,
):
    groups_t, groups_c = lax.axis_size("tm"), lax.axis_size("chan")
    held, slab = samples.shape
    assert slab // STRIDE == groups_c and groups_c % (2 * APART) == 0 and (groups_c // 2 * held) % ROWS == 0
    tokens = groups_c * held
    mates = groups_c // 2
    model = embed_weight.shape[1]
    flat = [w.reshape(w.shape[0] * w.shape[1], w.shape[2]) for w in (dilated_one, dilated_two, dilated_three, dilated_four)]
    width = SPAN * first_kernel.shape[1]
    anywhere = pl.BlockSpec(memory_space=pl.ANY)
    like = lambda w: pltpu.VMEM(w.shape, w.dtype)
    vmem = lambda *shape: pltpu.VMEM(shape, BF16)
    dma = pltpu.SemaphoreType.DMA
    return pl.pallas_call(
        functools.partial(kernel, groups_t, groups_c),
        out_shape=pltpu.VMEM((groups_c, held, model), BF16),
        in_specs=[anywhere] * 14,
        out_specs=anywhere,
        scratch_shapes=[
            vmem(groups_t, slab, held),
            vmem(groups_c, held, groups_t * slab),
            vmem(groups_t * slab, width),
            vmem(5 * dilated_one.shape[1], 2 * dilated_one.shape[2]),
            vmem(tokens, 128),
            vmem(ROWS, width),
            vmem(ROWS, 9 * 128),
            vmem(ROWS, 8 * 128),
            vmem(2 * ROWS, 3 * 256),
            vmem(2, tokens // 2, model),
            vmem(2, tokens // 2, model),
            vmem(2, tokens, model),
            vmem(2, tokens, model),
            vmem(ROWS, model),
            vmem(ROWS, up_weight.shape[1]),
            vmem(2, mates, held, model),
            pltpu.SMEM(dead_channels.shape, dead_channels.dtype),
            like(first_kernel),
            like(flat[0]),
            pltpu.VMEM((1, model), jnp.float32),
            pltpu.VMEM((1, model), jnp.float32),
        ]
        + [like(w) for w in flat[1:]]
        + [like(w) for w in (embed_weight, project_in, project_out, up_weight, down_weight)]
        + [
            dma((14,)),
            dma((groups_c,)),
            dma((groups_c,)),
            dma((groups_t,)),
            dma((groups_t,)),
            dma((2, mates)),
            dma((groups_c,)),
            dma((2,)),
        ],
        compiler_params=pltpu.CompilerParams(
            collective_id=0, has_side_effects=True, vmem_limit_bytes=44 * 2**20
        ),
    )(
        *[
            pltpu.with_memory_space_constraint(w, pltpu.HBM)
            for w in (
                dead_channels,
                samples.T,
                first_kernel,
                *flat,
                embed_weight,
                gain_one.reshape(1, -1),
                project_in,
                project_out,
                gain_two.reshape(1, -1),
                up_weight,
                down_weight,
            )
        ]
    )


def solution(mesh):
    return jax.shard_map(
        per_device,
        mesh=mesh,
        in_specs=(P("chan", "tm"), P(), P(), P(), P(), P(), P(), P(), P(), P(), P(), P(), P(), P()),
        out_specs=P("tm", "chan", None),
        check_vma=False,
    )
```

```python
import functools

import jax
import jax.numpy as jnp
from jax import lax
from jax.experimental import pallas as pl
from jax.experimental.pallas import tpu as pltpu
from jax.sharding import PartitionSpec as P

HEADS = 8
STRIDE = 4
EPSILON = 1e-05
REA256 = 15
APART = 4
SPAN = 2 * REA256 + APART + 2
ROWS = 192
MESH = pl.DeviceIdType.MESH
BF16 = jnp.bfloat16


def gelu(v, half=0.5):
    v = v.astype(BF16)
    scaled = v * jnp.asarray(half, BF16)
    return scaled + scaled * jnp.tanh(v * (BF16(0.7978845608028654) + BF16(0.035677408136300125) * (v * v)))


def dot(a, b):
    return jnp.dot(a, b, preferred_element_type=jnp.float32)


def dot_nt(a, b):
    return lax.dot_general(a, b, (((1,), (1,)), ((), ())), preferred_element_type=jnp.float32)


def normalize(tokens, gain):
    floats = tokens.astype(jnp.float32)
    centred = floats - jnp.mean(floats, axis=-1, keepdims=True)
    variance = jnp.mean(centred * centred, axis=-1, keepdims=True)
    return (centred * lax.rsqrt(variance + EPSILON) * gain).astype(BF16)


def staged(count, multiply, store, depth=1):
    ahead = [multiply(i) for i in range(min(depth, count))]
    for i in range(count):
        if i + depth < count:
            ahead.append(multiply(i + depth))
        store(i, ahead.pop(0))


def looped(count, body):
    if count == 1:
        body(0)
    else:
        lax.fori_loop(0, count, lambda i, c: (body(i), c)[1], 0)


def kernel(
    groups_t,
    groups_c,
    dead_hbm,
    samples_hbm,
    first_hbm,
    one_hbm,
    two_hbm,
    three_hbm,
    four_hbm,
    embed_hbm,
    gain_one_hbm,
    pin_hbm,
    pout_hbm,
    gain_two_hbm,
    up_hbm,
    down_hbm,
    out,
    raw,
    signal,
    toeplitz,
    one_wide,
    key_bias,
    h0,
    h1,
    h2,
    h3,
    embedded,
    queries,
    keys,
    values,
    attended,
    inner,
    result,
    dead,
    first_kernel,
    one,
    gain_one,
    gain_two,
    two,
    three,
    four,
    embed,
    pin,
    pout,
    up,
    down,
    weight_sem,
    send_sem,
    recv_sem,
    hand_send,
    hand_recv,
    out_send,
    out_recv,
    own_sem,
    far_ready,
):
    my_t, my_c = lax.axis_index("tm"), lax.axis_index("chan")
    slab, held = raw.shape[1:]
    total_samples = groups_t * slab
    frames = total_samples // STRIDE
    tokens = groups_c * held
    mates = groups_c // 2
    my_half, my_place = lax.div(my_c, mates), lax.rem(my_c, mates)

    def slot_of(place):
        return lax.div(place, APART) * (2 * APART) + lax.rem(place, APART)

    frame = my_t * (slab // STRIDE) + slot_of(my_place)

    barrier = pltpu.get_barrier_semaphore()

    def chan_peer(i):
        return lax.rem(my_c + 1 + i, groups_c)

    def mate(i):
        return my_half * mates + lax.rem(my_place + 1 + i, mates)

    def far_peer(i):
        return (1 - my_half) * mates + i

    def time_peer(i):
        return lax.rem(my_t + 1 + i, groups_t)

    def greet_mate(i):
        pl.semaphore_signal(barrier, inc=1, device_id=(my_t, mate(i)), device_id_type=MESH)

    def greet_far(i):
        pl.semaphore_signal(barrier, inc=1, device_id=(my_t, far_peer(i)), device_id_type=MESH)

    def answer_far(i):
        pl.semaphore_signal(far_ready, inc=1, device_id=(my_t, far_peer(i)), device_id_type=MESH)

    def greet_time(i):
        pl.semaphore_signal(barrier, inc=1, device_id=(time_peer(i), my_c), device_id_type=MESH)

    looped(groups_t - 1, greet_time)
    looped(mates - 1, greet_mate)

    @pl.when(my_half == 0)
    def _():
        looped(mates, greet_far)

    loads = [
        pltpu.make_async_copy(src, dst, weight_sem.at[i])
        for i, (src, dst) in enumerate(
            [
                (dead_hbm, dead),
                (samples_hbm, raw.at[my_t]),
                (first_hbm, first_kernel),
                (one_hbm, one),
                (gain_one_hbm, gain_one),
                (gain_two_hbm, gain_two),
                (two_hbm, two),
                (three_hbm, three),
                (four_hbm, four),
                (embed_hbm, embed),
                (pin_hbm, pin),
                (pout_hbm, pout),
                (up_hbm, up),
                (down_hbm, down),
            ]
        )
    ]
    for load in loads:
        load.start()

    @pl.when(my_half == 0)
    def _():
        pl.semaphore_wait(barrier, mates + groups_t - 2)

    @pl.when(my_half == 1)
    def _():
        pl.semaphore_wait(barrier, groups_c + groups_t - 2)

    def hand(peer, slab_at):
        return pltpu.make_async_remote_copy(
            src_ref=samples_hbm,
            dst_ref=raw.at[slab_at],
            send_sem=hand_send.at[peer],
            recv_sem=hand_recv.at[slab_at],
            device_id=(peer, my_c),
            device_id_type=MESH,
        )

    def spread(peer, slot):
        return pltpu.make_async_remote_copy(
            src_ref=signal.at[slot],
            dst_ref=signal.at[slot],
            send_sem=send_sem.at[peer],
            recv_sem=recv_sem.at[slot],
            device_id=(my_t, peer),
            device_id_type=MESH,
        )

    looped(groups_t - 1, lambda i: hand(time_peer(i), my_t).start())

    @pl.when(my_half == 1)
    def _():
        looped(mates, answer_far)

    for load in loads[:4]:
        load.wait()

    row_ids = lax.broadcasted_iota(jnp.int32, (held, held), 0)
    alive = row_ids == lax.broadcasted_iota(jnp.int32, (held, held), 1)
    row_ids = row_ids + my_c * held
    for i in range(dead.shape[0]):
        alive = jnp.logical_and(alive, row_ids != dead[i])
    alive = jnp.where(alive, 1.0, 0.0).astype(BF16)

    looped(groups_t - 1, lambda i: hand(time_peer(i), time_peer(i)).wait_recv())

    own = dot_nt(alive, raw[...].reshape(total_samples, held))
    signal[my_c] = own.astype(BF16)

    @pl.when(my_half == 1)
    def _():
        looped(mates, lambda i: spread(far_peer(i), my_c).start())

    looped(mates - 1, lambda i: spread(mate(i), my_c).start())

    c1 = first_kernel.shape[1]
    width = SPAN * c1
    pick = lax.broadcasted_iota(jnp.int32, (c1, width), 0) == lax.rem(
        lax.broadcasted_iota(jnp.int32, (c1, width), 1), c1
    )
    tiled = dot(first_kernel[...], pick.astype(jnp.float32).astype(BF16))
    c2 = one.shape[1]
    one_wide[...] = jnp.zeros_like(one_wide)
    one_wide[: 3 * c1, :c2] = one[...]
    one_wide[2 * c1 : 5 * c1, c2:] = one[...]

    for start in range(0, tokens, 384):
        shape = (384, 128)
        key_ids = lax.broadcasted_iota(jnp.int32, shape, 0) + start
        dead_keys = key_ids < 0
        for i in range(dead.shape[0]):
            dead_keys = jnp.logical_or(dead_keys, key_ids == dead[i])
        dead_keys = jnp.logical_and(dead_keys, lax.broadcasted_iota(jnp.int32, shape, 1) == 0)
        key_bias[start : start + 384, :] = jnp.where(dead_keys, -1e30, 0.0).astype(BF16)

    for start in range(0, total_samples, 128):
        size = min(128, total_samples - start)
        at_sample = lax.broadcasted_iota(jnp.int32, (size, width), 0) + start
        at_frame = lax.broadcasted_iota(jnp.int32, (size, width), 1) // c1 + (frame - REA256)
        tap = at_sample - STRIDE * at_frame + (first_kernel.shape[0] - STRIDE) // 2
        tap = jnp.where(jnp.logical_and(at_frame >= 0, at_frame < frames), tap, -1)
        band = jnp.zeros((size, width), jnp.float32)
        for k in range(first_kernel.shape[0]):
            band = jnp.where(tap == k, tiled[k : k + 1, :], band)
        toeplitz[start : start + size, :] = band.astype(BF16)

    @pl.when(my_half == 0)
    def _():
        pl.semaphore_wait(far_ready, mates)
        looped(mates, lambda i: spread(far_peer(i), my_c).start())

    def half_inside(offset):
        at = frame + offset
        return jnp.where(jnp.logical_and(at >= 0, at < frames), 0.5, 0.0)

    def flat_half(offset, lanes):
        return jnp.full((1, lanes), half_inside(offset), jnp.float32).astype(BF16)

    for load in loads[4:11]:
        load.wait()

    model = embed.shape[1]
    head = model // HEADS
    chans = ROWS // held
    half_blocks = mates // chans

    def convolve(mine, step):
        block = step + half_blocks * (my_half if mine else 1 - my_half)
        for i in range(chans):
            peer = block * chans + i

            @pl.when(peer != my_c)
            def _():
                spread(peer, peer).wait_recv()

        waves = signal[pl.ds(block * chans, chans)].reshape(ROWS, total_samples)
        for q in range(width // 384):
            cols = slice(q * 384, (q + 1) * 384)
            h0[:, cols] = gelu(dot(waves, toeplitz[:, cols]))
        later = lax.broadcasted_iota(jnp.int32, (1, 2 * c2), 1) >= c2
        for q in range(9):
            depth = min(5 * c1, width - 128 * q)
            keep = jnp.where(later, half_inside(4 * q + 2 - 14), half_inside(4 * q - 14)).astype(BF16)
            h1[:, 128 * q : 128 * (q + 1)] = gelu(dot(h0[:, 128 * q : 128 * q + depth], one_wide[:depth, :]), keep)
        for n in range(8):
            h2[:, 128 * n : 128 * (n + 1)] = gelu(
                dot(h1[:, 128 * n : 128 * n + 192], two[...]), flat_half(4 * n - 12, 128)
            )
        for k in range(2):
            for p in range(3):
                at = 256 * p + 128 * k
                h3[k * ROWS : (k + 1) * ROWS, 256 * p : 256 * (p + 1)] = gelu(
                    dot(h2[:, at : at + 384], three[...]), flat_half(APART * k + 8 * p - 8, 256)
                )
        rows = pl.ds(pl.multiple_of(block * ROWS, ROWS), ROWS)
        own_rows = pl.ds(pl.multiple_of(step * ROWS, ROWS), ROWS)
        parts = [slice(k * ROWS, (k + 1) * ROWS) for k in range(2)]
        features = [gelu(dot(h3[part, :], four[...])) for part in parts]
        tails = [dot(f, embed[...]).astype(BF16) for f in features]
        for k in range(2):
            normed = normalize(tails[k], gain_one[...])
            for q in range(model // 256):
                cols = slice(q * 256, (q + 1) * 256)
                keys[k, rows, cols] = dot(normed, pin[:, model + q * 256 : model + (q + 1) * 256]).astype(BF16)
                values[k, rows, cols] = dot(normed, pin[:, 2 * model + q * 256 : 2 * model + (q + 1) * 256]).astype(BF16)
            if mine:
                embedded[k, own_rows, :] = tails[k]
                for q in range(model // 256):
                    cols = slice(q * 256, (q + 1) * 256)
                    queries[k, own_rows, cols] = (dot(normed, pin[:, cols]).astype(BF16).astype(jnp.float32) * (head**-0.5)).astype(BF16)

    looped(half_blocks, functools.partial(convolve, True))
    looped(half_blocks, functools.partial(convolve, False))

    for load in loads[11:]:
        load.wait()

    def back(k, place):
        return pltpu.make_async_remote_copy(
            src_ref=result.at[k, place],
            dst_ref=out.at[slot_of(my_place) + APART * k],
            send_sem=out_send.at[k, place],
            recv_sem=out_recv.at[slot_of(my_place) + APART * k],
            device_id=(my_t, my_half * mates + place),
            device_id_type=MESH,
        )

    def keep_own(k):
        return pltpu.make_async_copy(
            result.at[k, my_place], out.at[slot_of(my_place) + APART * k], own_sem.at[k]
        )

    def encode(k, step):
        rows = pl.ds(pl.multiple_of(step * ROWS, ROWS), ROWS)
        first_head = lax.broadcasted_iota(jnp.int32, (1, 2 * head), 1) < head
        unit = (lax.broadcasted_iota(jnp.int32, (2 * ROWS, 128), 1) == 0).astype(jnp.float32).astype(BF16)
        ones = jnp.ones((tokens, 128), BF16)
        nothing = jnp.zeros((ROWS, 2 * head), BF16)
        def score(base):
            cols = slice(base, base + 2 * head)
            pair = queries[k, rows, cols]
            stacked = jnp.concatenate(
                [jnp.where(first_head, pair, nothing), jnp.where(first_head, nothing, pair)], axis=0
            )
            return dot_nt(
                jnp.concatenate([stacked, unit], axis=1), jnp.concatenate([keys[k, :, cols], key_bias[...]], axis=1)
            )

        ahead = score(0)
        for base in range(0, model, 2 * head):
            cols = slice(base, base + 2 * head)
            scores = ahead
            if base + 2 * head < model:
                ahead = score(base + 2 * head)
            exponent = jnp.exp((scores - jnp.max(scores, axis=1, keepdims=True)).astype(BF16))
            mean = dot(exponent, jnp.concatenate([values[k, :, cols], ones], axis=1))
            summed = jnp.where(first_head, mean[:ROWS, :128], mean[ROWS:, :128])
            total = jnp.where(first_head, mean[:ROWS, 128:], mean[ROWS:, 128:])
            attended[:, cols] = (summed / total).astype(BF16)
        mixed = (embedded[k, rows, :].astype(jnp.float32) + dot(attended[...], pout[...])).astype(BF16)
        normed = normalize(mixed, gain_two[...])
        def save_inner(q, part):
            inner[:, 256 * q : 256 * (q + 1)] = gelu(part)

        staged(up.shape[1] // 256, lambda q: dot(normed, up[:, 256 * q : 256 * (q + 1)]), save_inner)
        total = mixed.astype(jnp.float32) + dot(inner[...], down[...])
        result[k, pl.ds(step * chans, chans)] = total.astype(BF16).reshape(chans, held, model)

    for k in range(2):
        looped(half_blocks, functools.partial(encode, k))
        looped(mates - 1, lambda i: back(k, lax.rem(my_place + 1 + i, mates)).start())
        keep_own(k).start()

    looped(groups_t - 1, lambda i: hand(time_peer(i), my_t).wait_send())
    looped(groups_c - 1, lambda i: spread(chan_peer(i), my_c).wait_send())

    for k in range(2):

        def finish(i):
            place = lax.rem(my_place + 1 + i, mates)
            back(k, place).wait_send()
            at = slot_of(place) + APART * k
            pltpu.make_async_remote_copy(
                src_ref=result.at[k, place],
                dst_ref=out.at[at],
                send_sem=out_send.at[k, place],
                recv_sem=out_recv.at[at],
                device_id=(my_t, my_half * mates + place),
                device_id_type=MESH,
            ).wait_recv()

        looped(mates - 1, finish)
        keep_own(k).wait()


def per_device(
    samples,
    dead_channels,
    first_kernel,
    dilated_one,
    dilated_two,
    dilated_three,
    dilated_four,
    embed_weight,
    gain_one,
    project_in,
    project_out,
    gain_two,
    up_weight,
    down_weight,
):
    groups_t, groups_c = lax.axis_size("tm"), lax.axis_size("chan")
    held, slab = samples.shape
    assert slab // STRIDE == groups_c and groups_c % (2 * APART) == 0 and (groups_c // 2 * held) % ROWS == 0
    tokens = groups_c * held
    mates = groups_c // 2
    model = embed_weight.shape[1]
    flat = [w.reshape(w.shape[0] * w.shape[1], w.shape[2]) for w in (dilated_one, dilated_two, dilated_three, dilated_four)]
    width = SPAN * first_kernel.shape[1]
    anywhere = pl.BlockSpec(memory_space=pl.ANY)
    like = lambda w: pltpu.VMEM(w.shape, w.dtype)
    vmem = lambda *shape: pltpu.VMEM(shape, BF16)
    dma = pltpu.SemaphoreType.DMA
    return pl.pallas_call(
        functools.partial(kernel, groups_t, groups_c),
        out_shape=pltpu.VMEM((groups_c, held, model), BF16),
        in_specs=[anywhere] * 14,
        out_specs=anywhere,
        scratch_shapes=[
            vmem(groups_t, slab, held),
            vmem(groups_c, held, groups_t * slab),
            vmem(groups_t * slab, width),
            vmem(5 * dilated_one.shape[1], 2 * dilated_one.shape[2]),
            vmem(tokens, 128),
            vmem(ROWS, width),
            vmem(ROWS, 9 * 128),
            vmem(ROWS, 8 * 128),
            vmem(2 * ROWS, 3 * 256),
            vmem(2, tokens // 2, model),
            vmem(2, tokens // 2, model),
            vmem(2, tokens, model),
            vmem(2, tokens, model),
            vmem(ROWS, model),
            vmem(ROWS, up_weight.shape[1]),
            vmem(2, mates, held, model),
            pltpu.SMEM(dead_channels.shape, dead_channels.dtype),
            like(first_kernel),
            like(flat[0]),
            pltpu.VMEM((1, model), jnp.float32),
            pltpu.VMEM((1, model), jnp.float32),
        ]
        + [like(w) for w in flat[1:]]
        + [like(w) for w in (embed_weight, project_in, project_out, up_weight, down_weight)]
        + [
            dma((14,)),
            dma((groups_c,)),
            dma((groups_c,)),
            dma((groups_t,)),
            dma((groups_t,)),
            dma((2, mates)),
            dma((groups_c,)),
            dma((2,)),
            pltpu.SemaphoreType.REGULAR,
        ],
        compiler_params=pltpu.CompilerParams(
            collective_id=0, has_side_effects=True, vmem_limit_bytes=44 * 2**20
        ),
    )(
        *[
            pltpu.with_memory_space_constraint(w, pltpu.HBM)
            for w in (
                dead_channels,
                samples.T,
                first_kernel,
                *flat,
                embed_weight,
                gain_one.reshape(1, -1),
                project_in,
                project_out,
                gain_two.reshape(1, -1),
                up_weight,
                down_weight,
            )
        ]
    )


def solution(mesh):
    return jax.shard_map(
        per_device,
        mesh=mesh,
        in_specs=(P("chan", "tm"), P(), P(), P(), P(), P(), P(), P(), P(), P(), P(), P(), P(), P()),
        out_specs=P("tm", "chan", None),
        check_vma=False,
    )
```

```python
import functools

import jax
import jax.numpy as jnp
from jax import lax
from jax.experimental import pallas as pl
from jax.experimental.pallas import tpu as pltpu
from jax.sharding import PartitionSpec as P

HEADS = 8
STRIDE = 4
EPSILON = 1e-05
REA256 = 15
APART = 4
SPAN = 2 * REA256 + APART + 2
ROWS = 192
MESH = pl.DeviceIdType.MESH
BF16 = jnp.bfloat16


def gelu(v, half=0.5):
    v = v.astype(BF16)
    scaled = v * jnp.asarray(half, BF16)
    return scaled + scaled * jnp.tanh(v * (BF16(0.7978845608028654) + BF16(0.035677408136300125) * (v * v)))


def dot(a, b):
    return jnp.dot(a, b, preferred_element_type=jnp.float32)


def dot_nt(a, b):
    return lax.dot_general(a, b, (((1,), (1,)), ((), ())), preferred_element_type=jnp.float32)


def normalize(tokens, gain):
    floats = tokens.astype(jnp.float32)
    centred = floats - jnp.mean(floats, axis=-1, keepdims=True)
    variance = jnp.mean(centred * centred, axis=-1, keepdims=True)
    return (centred * lax.rsqrt(variance + EPSILON) * gain).astype(BF16)


def staged(count, multiply, store, depth=1):
    ahead = [multiply(i) for i in range(min(depth, count))]
    for i in range(count):
        if i + depth < count:
            ahead.append(multiply(i + depth))
        store(i, ahead.pop(0))


def looped(count, body):
    if count == 1:
        body(0)
    else:
        lax.fori_loop(0, count, lambda i, c: (body(i), c)[1], 0)


def kernel(
    groups_t,
    groups_c,
    dead_hbm,
    samples_hbm,
    first_hbm,
    one_hbm,
    two_hbm,
    three_hbm,
    four_hbm,
    embed_hbm,
    gain_one_hbm,
    pin_hbm,
    pout_hbm,
    gain_two_hbm,
    up_hbm,
    down_hbm,
    out,
    raw,
    signal,
    toeplitz,
    one_wide,
    key_bias,
    h0,
    h1,
    h2,
    h3,
    embedded,
    queries,
    keys,
    values,
    attended,
    inner,
    result,
    dead,
    first_kernel,
    one,
    gain_one,
    gain_two,
    two,
    three,
    four,
    embed,
    pin,
    pout,
    up,
    down,
    weight_sem,
    send_sem,
    recv_sem,
    hand_send,
    hand_recv,
    out_send,
    out_recv,
    own_sem,
    far_ready,
):
    my_t, my_c = lax.axis_index("tm"), lax.axis_index("chan")
    slab, held = raw.shape[1:]
    total_samples = groups_t * slab
    frames = total_samples // STRIDE
    tokens = groups_c * held
    mates = groups_c // 2
    my_half, my_place = lax.div(my_c, mates), lax.rem(my_c, mates)

    def slot_of(place):
        return lax.div(place, APART) * (2 * APART) + lax.rem(place, APART)

    frame = my_t * (slab // STRIDE) + slot_of(my_place)

    barrier = pltpu.get_barrier_semaphore()

    def chan_peer(i):
        return lax.rem(my_c + 1 + i, groups_c)

    def mate(i):
        return my_half * mates + lax.rem(my_place + 1 + i, mates)

    def far_peer(i):
        return (1 - my_half) * mates + i

    def time_peer(i):
        return lax.rem(my_t + 1 + i, groups_t)

    def greet_mate(i):
        pl.semaphore_signal(barrier, inc=1, device_id=(my_t, mate(i)), device_id_type=MESH)

    def greet_far(i):
        pl.semaphore_signal(barrier, inc=1, device_id=(my_t, far_peer(i)), device_id_type=MESH)

    def answer_far(i):
        pl.semaphore_signal(far_ready, inc=1, device_id=(my_t, far_peer(i)), device_id_type=MESH)

    def greet_time(i):
        pl.semaphore_signal(barrier, inc=1, device_id=(time_peer(i), my_c), device_id_type=MESH)

    looped(groups_t - 1, greet_time)
    looped(mates - 1, greet_mate)

    @pl.when(my_half == 0)
    def _():
        looped(mates, greet_far)

    loads = [
        pltpu.make_async_copy(src, dst, weight_sem.at[i])
        for i, (src, dst) in enumerate(
            [
                (dead_hbm, dead),
                (samples_hbm, raw.at[my_t]),
                (first_hbm, first_kernel),
                (one_hbm, one),
                (gain_one_hbm, gain_one),
                (gain_two_hbm, gain_two),
                (two_hbm, two),
                (three_hbm, three),
                (four_hbm, four),
                (embed_hbm, embed),
                (pin_hbm, pin),
                (pout_hbm, pout),
                (up_hbm, up),
                (down_hbm, down),
            ]
        )
    ]
    for load in loads:
        load.start()

    @pl.when(my_half == 0)
    def _():
        pl.semaphore_wait(barrier, mates + groups_t - 2)

    @pl.when(my_half == 1)
    def _():
        pl.semaphore_wait(barrier, groups_c + groups_t - 2)

    def hand(peer, slab_at):
        return pltpu.make_async_remote_copy(
            src_ref=samples_hbm,
            dst_ref=raw.at[slab_at],
            send_sem=hand_send.at[peer],
            recv_sem=hand_recv.at[slab_at],
            device_id=(peer, my_c),
            device_id_type=MESH,
        )

    def spread(peer, slot):
        return pltpu.make_async_remote_copy(
            src_ref=signal.at[slot],
            dst_ref=signal.at[slot],
            send_sem=send_sem.at[peer],
            recv_sem=recv_sem.at[slot],
            device_id=(my_t, peer),
            device_id_type=MESH,
        )

    looped(groups_t - 1, lambda i: hand(time_peer(i), my_t).start())

    @pl.when(my_half == 1)
    def _():
        looped(mates, answer_far)

    for load in loads[:4]:
        load.wait()

    row_ids = lax.broadcasted_iota(jnp.int32, (held, held), 0)
    alive = row_ids == lax.broadcasted_iota(jnp.int32, (held, held), 1)
    row_ids = row_ids + my_c * held
    for i in range(dead.shape[0]):
        alive = jnp.logical_and(alive, row_ids != dead[i])
    alive = jnp.where(alive, 1.0, 0.0).astype(BF16)

    looped(groups_t - 1, lambda i: hand(time_peer(i), time_peer(i)).wait_recv())

    own = dot_nt(alive, raw[...].reshape(total_samples, held))
    signal[my_c] = own.astype(BF16)

    @pl.when(my_half == 1)
    def _():
        looped(mates, lambda i: spread(far_peer(i), my_c).start())

    looped(mates - 1, lambda i: spread(mate(i), my_c).start())

    c1 = first_kernel.shape[1]
    width = SPAN * c1
    pick = lax.broadcasted_iota(jnp.int32, (c1, width), 0) == lax.rem(
        lax.broadcasted_iota(jnp.int32, (c1, width), 1), c1
    )
    tiled = dot(first_kernel[...], pick.astype(jnp.float32).astype(BF16))
    c2 = one.shape[1]
    one_wide[...] = jnp.zeros_like(one_wide)
    one_wide[: 3 * c1, :c2] = one[...]
    one_wide[2 * c1 : 5 * c1, c2:] = one[...]

    for start in range(0, tokens, 384):
        shape = (384, 128)
        key_ids = lax.broadcasted_iota(jnp.int32, shape, 0) + start
        dead_keys = key_ids < 0
        for i in range(dead.shape[0]):
            dead_keys = jnp.logical_or(dead_keys, key_ids == dead[i])
        dead_keys = jnp.logical_and(dead_keys, lax.broadcasted_iota(jnp.int32, shape, 1) == 0)
        key_bias[start : start + 384, :] = jnp.where(dead_keys, -1e30, 0.0).astype(BF16)

    for start in range(0, total_samples, 128):
        size = min(128, total_samples - start)
        at_sample = lax.broadcasted_iota(jnp.int32, (size, width), 0) + start
        at_frame = lax.broadcasted_iota(jnp.int32, (size, width), 1) // c1 + (frame - REA256)
        tap = at_sample - STRIDE * at_frame + (first_kernel.shape[0] - STRIDE) // 2
        tap = jnp.where(jnp.logical_and(at_frame >= 0, at_frame < frames), tap, -1)
        band = jnp.zeros((size, width), jnp.float32)
        for k in range(first_kernel.shape[0]):
            band = jnp.where(tap == k, tiled[k : k + 1, :], band)
        toeplitz[start : start + size, :] = band.astype(BF16)

    @pl.when(my_half == 0)
    def _():
        pl.semaphore_wait(far_ready, mates)
        looped(mates, lambda i: spread(far_peer(i), my_c).start())

    def half_inside(offset):
        at = frame + offset
        return jnp.where(jnp.logical_and(at >= 0, at < frames), 0.5, 0.0)

    def flat_half(offset, lanes):
        return jnp.full((1, lanes), half_inside(offset), jnp.float32).astype(BF16)

    for load in loads[4:11]:
        load.wait()

    model = embed.shape[1]
    head = model // HEADS
    chans = ROWS // held
    half_blocks = mates // chans

    def convolve(mine, step):
        block = step + half_blocks * (my_half if mine else 1 - my_half)
        for i in range(chans):
            peer = block * chans + i

            @pl.when(peer != my_c)
            def _():
                spread(peer, peer).wait_recv()

        waves = signal[pl.ds(block * chans, chans)].reshape(ROWS, total_samples)
        for q in range(width // 384):
            cols = slice(q * 384, (q + 1) * 384)
            h0[:, cols] = gelu(dot(waves, toeplitz[:, cols]))
        later = lax.broadcasted_iota(jnp.int32, (1, 2 * c2), 1) >= c2
        for q in range(9):
            depth = min(5 * c1, width - 128 * q)
            keep = jnp.where(later, half_inside(4 * q + 2 - 14), half_inside(4 * q - 14)).astype(BF16)
            h1[:, 128 * q : 128 * (q + 1)] = gelu(dot(h0[:, 128 * q : 128 * q + depth], one_wide[:depth, :]), keep)
        for n in range(8):
            h2[:, 128 * n : 128 * (n + 1)] = gelu(
                dot(h1[:, 128 * n : 128 * n + 192], two[...]), flat_half(4 * n - 12, 128)
            )
        for k in range(2):
            for p in range(3):
                at = 256 * p + 128 * k
                h3[k * ROWS : (k + 1) * ROWS, 256 * p : 256 * (p + 1)] = gelu(
                    dot(h2[:, at : at + 384], three[...]), flat_half(APART * k + 8 * p - 8, 256)
                )
        rows = pl.ds(pl.multiple_of(block * ROWS, ROWS), ROWS)
        own_rows = pl.ds(pl.multiple_of(step * ROWS, ROWS), ROWS)
        parts = [slice(k * ROWS, (k + 1) * ROWS) for k in range(2)]
        features = [gelu(dot(h3[part, :], four[...])) for part in parts]
        tails = [dot(f, embed[...]).astype(BF16) for f in features]
        for k in range(2):
            normed = normalize(tails[k], gain_one[...])
            for q in range(model // 256):
                cols = slice(q * 256, (q + 1) * 256)
                keys[k, rows, cols] = dot(normed, pin[:, model + q * 256 : model + (q + 1) * 256]).astype(BF16)
                values[k, rows, cols] = dot(normed, pin[:, 2 * model + q * 256 : 2 * model + (q + 1) * 256]).astype(BF16)
            if mine:
                embedded[k, own_rows, :] = tails[k]
                for q in range(model // 256):
                    cols = slice(q * 256, (q + 1) * 256)
                    queries[k, own_rows, cols] = (dot(normed, pin[:, cols]).astype(BF16).astype(jnp.float32) * (head**-0.5)).astype(BF16)

    looped(half_blocks, functools.partial(convolve, True))
    looped(half_blocks, functools.partial(convolve, False))

    for load in loads[11:]:
        load.wait()

    def back(k, place):
        return pltpu.make_async_remote_copy(
            src_ref=result.at[k, place],
            dst_ref=out.at[slot_of(my_place) + APART * k],
            send_sem=out_send.at[k, place],
            recv_sem=out_recv.at[slot_of(my_place) + APART * k],
            device_id=(my_t, my_half * mates + place),
            device_id_type=MESH,
        )

    def keep_own(k):
        return pltpu.make_async_copy(
            result.at[k, my_place], out.at[slot_of(my_place) + APART * k], own_sem.at[k]
        )

    def encode(k, step):
        rows = pl.ds(pl.multiple_of(step * ROWS, ROWS), ROWS)
        first_head = lax.broadcasted_iota(jnp.int32, (1, 2 * head), 1) < head
        unit = (lax.broadcasted_iota(jnp.int32, (2 * ROWS, 128), 1) == 0).astype(jnp.float32).astype(BF16)
        ones = jnp.ones((tokens, 128), BF16)
        nothing = jnp.zeros((ROWS, 2 * head), BF16)
        def score(base):
            cols = slice(base, base + 2 * head)
            pair = queries[k, rows, cols]
            stacked = jnp.concatenate(
                [jnp.where(first_head, pair, nothing), jnp.where(first_head, nothing, pair)], axis=0
            )
            return dot_nt(
                jnp.concatenate([stacked, unit], axis=1), jnp.concatenate([keys[k, :, cols], key_bias[...]], axis=1)
            )

        def save(i, scores):
            cols = slice(2 * head * i, 2 * head * (i + 1))
            exponent = jnp.exp((scores - jnp.max(scores, axis=1, keepdims=True)).astype(BF16))
            mean = dot(exponent, jnp.concatenate([values[k, :, cols], ones], axis=1))
            summed = jnp.where(first_head, mean[:ROWS, :128], mean[ROWS:, :128])
            total = jnp.where(first_head, mean[:ROWS, 128:], mean[ROWS:, 128:])
            attended[:, cols] = (summed / total).astype(BF16)

        staged(model // (2 * head), lambda i: score(2 * head * i), save, 4)
        mixed = (embedded[k, rows, :].astype(jnp.float32) + dot(attended[...], pout[...])).astype(BF16)
        normed = normalize(mixed, gain_two[...])
        def save_inner(q, part):
            inner[:, 256 * q : 256 * (q + 1)] = gelu(part)

        staged(up.shape[1] // 256, lambda q: dot(normed, up[:, 256 * q : 256 * (q + 1)]), save_inner)
        total = mixed.astype(jnp.float32) + dot(inner[...], down[...])
        result[k, pl.ds(step * chans, chans)] = total.astype(BF16).reshape(chans, held, model)

    for k in range(2):
        looped(half_blocks, functools.partial(encode, k))
        looped(mates - 1, lambda i: back(k, lax.rem(my_place + 1 + i, mates)).start())
        keep_own(k).start()

    looped(groups_t - 1, lambda i: hand(time_peer(i), my_t).wait_send())
    looped(groups_c - 1, lambda i: spread(chan_peer(i), my_c).wait_send())

    for k in range(2):

        def finish(i):
            place = lax.rem(my_place + 1 + i, mates)
            back(k, place).wait_send()
            at = slot_of(place) + APART * k
            pltpu.make_async_remote_copy(
                src_ref=result.at[k, place],
                dst_ref=out.at[at],
                send_sem=out_send.at[k, place],
                recv_sem=out_recv.at[at],
                device_id=(my_t, my_half * mates + place),
                device_id_type=MESH,
            ).wait_recv()

        looped(mates - 1, finish)
        keep_own(k).wait()


def per_device(
    samples,
    dead_channels,
    first_kernel,
    dilated_one,
    dilated_two,
    dilated_three,
    dilated_four,
    embed_weight,
    gain_one,
    project_in,
    project_out,
    gain_two,
    up_weight,
    down_weight,
):
    groups_t, groups_c = lax.axis_size("tm"), lax.axis_size("chan")
    held, slab = samples.shape
    assert slab // STRIDE == groups_c and groups_c % (2 * APART) == 0 and (groups_c // 2 * held) % ROWS == 0
    tokens = groups_c * held
    mates = groups_c // 2
    model = embed_weight.shape[1]
    flat = [w.reshape(w.shape[0] * w.shape[1], w.shape[2]) for w in (dilated_one, dilated_two, dilated_three, dilated_four)]
    width = SPAN * first_kernel.shape[1]
    anywhere = pl.BlockSpec(memory_space=pl.ANY)
    like = lambda w: pltpu.VMEM(w.shape, w.dtype)
    vmem = lambda *shape: pltpu.VMEM(shape, BF16)
    dma = pltpu.SemaphoreType.DMA
    return pl.pallas_call(
        functools.partial(kernel, groups_t, groups_c),
        out_shape=pltpu.VMEM((groups_c, held, model), BF16),
        in_specs=[anywhere] * 14,
        out_specs=anywhere,
        scratch_shapes=[
            vmem(groups_t, slab, held),
            vmem(groups_c, held, groups_t * slab),
            vmem(groups_t * slab, width),
            vmem(5 * dilated_one.shape[1], 2 * dilated_one.shape[2]),
            vmem(tokens, 128),
            vmem(ROWS, width),
            vmem(ROWS, 9 * 128),
            vmem(ROWS, 8 * 128),
            vmem(2 * ROWS, 3 * 256),
            vmem(2, tokens // 2, model),
            vmem(2, tokens // 2, model),
            vmem(2, tokens, model),
            vmem(2, tokens, model),
            vmem(ROWS, model),
            vmem(ROWS, up_weight.shape[1]),
            vmem(2, mates, held, model),
            pltpu.SMEM(dead_channels.shape, dead_channels.dtype),
            like(first_kernel),
            like(flat[0]),
            pltpu.VMEM((1, model), jnp.float32),
            pltpu.VMEM((1, model), jnp.float32),
        ]
        + [like(w) for w in flat[1:]]
        + [like(w) for w in (embed_weight, project_in, project_out, up_weight, down_weight)]
        + [
            dma((14,)),
            dma((groups_c,)),
            dma((groups_c,)),
            dma((groups_t,)),
            dma((groups_t,)),
            dma((2, mates)),
            dma((groups_c,)),
            dma((2,)),
            pltpu.SemaphoreType.REGULAR,
        ],
        compiler_params=pltpu.CompilerParams(
            collective_id=0, has_side_effects=True, vmem_limit_bytes=44 * 2**20
        ),
    )(
        *[
            pltpu.with_memory_space_constraint(w, pltpu.HBM)
            for w in (
                dead_channels,
                samples.T,
                first_kernel,
                *flat,
                embed_weight,
                gain_one.reshape(1, -1),
                project_in,
                project_out,
                gain_two.reshape(1, -1),
                up_weight,
                down_weight,
            )
        ]
    )


def solution(mesh):
    return jax.shard_map(
        per_device,
        mesh=mesh,
        in_specs=(P("chan", "tm"), P(), P(), P(), P(), P(), P(), P(), P(), P(), P(), P(), P(), P()),
        out_specs=P("tm", "chan", None),
        check_vma=False,
    )
```

```python
import functools

import jax
import jax.numpy as jnp
from jax import lax
from jax.experimental import pallas as pl
from jax.experimental.pallas import tpu as pltpu
from jax.sharding import PartitionSpec as P

HEADS = 8
STRIDE = 4
EPSILON = 1e-05
REA256 = 15
APART = 4
SPAN = 2 * REA256 + APART + 2
ROWS = 192
MESH = pl.DeviceIdType.MESH
BF16 = jnp.bfloat16


def gelu(v, half=0.5):
    v = v.astype(BF16)
    scaled = v * jnp.asarray(half, BF16)
    return scaled + scaled * jnp.tanh(v * (BF16(0.7978845608028654) + BF16(0.035677408136300125) * (v * v)))


def dot(a, b):
    return jnp.dot(a, b, preferred_element_type=jnp.float32)


def dot_nt(a, b):
    return lax.dot_general(a, b, (((1,), (1,)), ((), ())), preferred_element_type=jnp.float32)


def normalize(tokens, gain):
    floats = tokens.astype(jnp.float32)
    centred = floats - jnp.mean(floats, axis=-1, keepdims=True)
    variance = jnp.mean(centred * centred, axis=-1, keepdims=True)
    return (centred * lax.rsqrt(variance + EPSILON) * gain).astype(BF16)


def staged(count, multiply, store, depth=1):
    ahead = [multiply(i) for i in range(min(depth, count))]
    for i in range(count):
        if i + depth < count:
            ahead.append(multiply(i + depth))
        store(i, ahead.pop(0))


def looped(count, body):
    if count == 1:
        body(0)
    else:
        lax.fori_loop(0, count, lambda i, c: (body(i), c)[1], 0)


def kernel(
    groups_t,
    groups_c,
    dead_hbm,
    samples_hbm,
    first_hbm,
    one_hbm,
    two_hbm,
    three_hbm,
    four_hbm,
    embed_hbm,
    gain_one_hbm,
    pin_hbm,
    pout_hbm,
    gain_two_hbm,
    up_hbm,
    down_hbm,
    out,
    raw,
    signal,
    toeplitz,
    one_wide,
    key_bias,
    h0,
    h1,
    h2,
    h3,
    embedded,
    queries,
    keys,
    values,
    attended,
    inner,
    result,
    dead,
    first_kernel,
    one,
    gain_one,
    gain_two,
    two,
    three,
    four,
    embed,
    pin,
    pout,
    up,
    down,
    weight_sem,
    send_sem,
    recv_sem,
    hand_send,
    hand_recv,
    out_send,
    out_recv,
    own_sem,
    far_ready,
):
    my_t, my_c = lax.axis_index("tm"), lax.axis_index("chan")
    slab, held = raw.shape[1:]
    total_samples = groups_t * slab
    frames = total_samples // STRIDE
    tokens = groups_c * held
    mates = groups_c // 2
    my_half, my_place = lax.div(my_c, mates), lax.rem(my_c, mates)

    def slot_of(place):
        return lax.div(place, APART) * (2 * APART) + lax.rem(place, APART)

    frame = my_t * (slab // STRIDE) + slot_of(my_place)

    barrier = pltpu.get_barrier_semaphore()

    def chan_peer(i):
        return lax.rem(my_c + 1 + i, groups_c)

    def mate(i):
        return my_half * mates + lax.rem(my_place + 1 + i, mates)

    def far_peer(i):
        return (1 - my_half) * mates + i

    def time_peer(i):
        return lax.rem(my_t + 1 + i, groups_t)

    def greet_mate(i):
        pl.semaphore_signal(barrier, inc=1, device_id=(my_t, mate(i)), device_id_type=MESH)

    def greet_far(i):
        pl.semaphore_signal(barrier, inc=1, device_id=(my_t, far_peer(i)), device_id_type=MESH)

    def answer_far(i):
        pl.semaphore_signal(far_ready, inc=1, device_id=(my_t, far_peer(i)), device_id_type=MESH)

    def greet_time(i):
        pl.semaphore_signal(barrier, inc=1, device_id=(time_peer(i), my_c), device_id_type=MESH)

    looped(groups_t - 1, greet_time)
    looped(mates - 1, greet_mate)

    @pl.when(my_half == 0)
    def _():
        looped(mates, greet_far)

    loads = [
        pltpu.make_async_copy(src, dst, weight_sem.at[i])
        for i, (src, dst) in enumerate(
            [
                (dead_hbm, dead),
                (samples_hbm, raw.at[my_t]),
                (first_hbm, first_kernel),
                (one_hbm, one),
                (gain_one_hbm, gain_one),
                (gain_two_hbm, gain_two),
                (two_hbm, two),
                (three_hbm, three),
                (four_hbm, four),
                (embed_hbm, embed),
                (pin_hbm, pin),
                (pout_hbm, pout),
                (up_hbm, up),
                (down_hbm, down),
            ]
        )
    ]
    for load in loads:
        load.start()

    c1 = first_kernel.shape[1]
    width = SPAN * c1
    c2 = one.shape[1]

    def prepare():
        pick = lax.broadcasted_iota(jnp.int32, (c1, width), 0) == lax.rem(
            lax.broadcasted_iota(jnp.int32, (c1, width), 1), c1
        )
        tiled = dot(first_kernel[...], pick.astype(jnp.float32).astype(BF16))
        one_wide[...] = jnp.zeros_like(one_wide)
        one_wide[: 3 * c1, :c2] = one[...]
        one_wide[2 * c1 : 5 * c1, c2:] = one[...]

        for start in range(0, tokens, 384):
            shape = (384, 128)
            key_ids = lax.broadcasted_iota(jnp.int32, shape, 0) + start
            dead_keys = key_ids < 0
            for i in range(dead.shape[0]):
                dead_keys = jnp.logical_or(dead_keys, key_ids == dead[i])
            dead_keys = jnp.logical_and(dead_keys, lax.broadcasted_iota(jnp.int32, shape, 1) == 0)
            key_bias[start : start + 384, :] = jnp.where(dead_keys, -1e30, 0.0).astype(BF16)

        for start in range(0, total_samples, 128):
            size = min(128, total_samples - start)
            at_sample = lax.broadcasted_iota(jnp.int32, (size, width), 0) + start
            at_frame = lax.broadcasted_iota(jnp.int32, (size, width), 1) // c1 + (frame - REA256)
            tap = at_sample - STRIDE * at_frame + (first_kernel.shape[0] - STRIDE) // 2
            tap = jnp.where(jnp.logical_and(at_frame >= 0, at_frame < frames), tap, -1)
            band = jnp.zeros((size, width), jnp.float32)
            for k in range(first_kernel.shape[0]):
                band = jnp.where(tap == k, tiled[k : k + 1, :], band)
            toeplitz[start : start + size, :] = band.astype(BF16)

    @pl.when(my_half == 0)
    def _():
        for load in loads[:4]:
            load.wait()
        prepare()
        pl.semaphore_wait(barrier, mates + groups_t - 2)

    @pl.when(my_half == 1)
    def _():
        pl.semaphore_wait(barrier, groups_c + groups_t - 2)

    def hand(peer, slab_at):
        return pltpu.make_async_remote_copy(
            src_ref=samples_hbm,
            dst_ref=raw.at[slab_at],
            send_sem=hand_send.at[peer],
            recv_sem=hand_recv.at[slab_at],
            device_id=(peer, my_c),
            device_id_type=MESH,
        )

    def spread(peer, slot):
        return pltpu.make_async_remote_copy(
            src_ref=signal.at[slot],
            dst_ref=signal.at[slot],
            send_sem=send_sem.at[peer],
            recv_sem=recv_sem.at[slot],
            device_id=(my_t, peer),
            device_id_type=MESH,
        )

    looped(groups_t - 1, lambda i: hand(time_peer(i), my_t).start())

    @pl.when(my_half == 1)
    def _():
        looped(mates, answer_far)

    @pl.when(my_half == 1)
    def _():
        for load in loads[:4]:
            load.wait()

    row_ids = lax.broadcasted_iota(jnp.int32, (held, held), 0)
    alive = row_ids == lax.broadcasted_iota(jnp.int32, (held, held), 1)
    row_ids = row_ids + my_c * held
    for i in range(dead.shape[0]):
        alive = jnp.logical_and(alive, row_ids != dead[i])
    alive = jnp.where(alive, 1.0, 0.0).astype(BF16)

    looped(groups_t - 1, lambda i: hand(time_peer(i), time_peer(i)).wait_recv())

    own = dot_nt(alive, raw[...].reshape(total_samples, held))
    signal[my_c] = own.astype(BF16)

    @pl.when(my_half == 1)
    def _():
        looped(mates, lambda i: spread(far_peer(i), my_c).start())

    looped(mates - 1, lambda i: spread(mate(i), my_c).start())

    @pl.when(my_half == 1)
    def _():
        prepare()

    @pl.when(my_half == 0)
    def _():
        pl.semaphore_wait(far_ready, mates)
        looped(mates, lambda i: spread(far_peer(i), my_c).start())

    def half_inside(offset):
        at = frame + offset
        return jnp.where(jnp.logical_and(at >= 0, at < frames), 0.5, 0.0)

    def flat_half(offset, lanes):
        return jnp.full((1, lanes), half_inside(offset), jnp.float32).astype(BF16)

    for load in loads[4:11]:
        load.wait()

    model = embed.shape[1]
    head = model // HEADS
    chans = ROWS // held
    half_blocks = mates // chans

    def convolve(mine, step):
        block = step + half_blocks * (my_half if mine else 1 - my_half)
        for i in range(chans):
            peer = block * chans + i

            @pl.when(peer != my_c)
            def _():
                spread(peer, peer).wait_recv()

        waves = signal[pl.ds(block * chans, chans)].reshape(ROWS, total_samples)
        for q in range(width // 384):
            cols = slice(q * 384, (q + 1) * 384)
            h0[:, cols] = gelu(dot(waves, toeplitz[:, cols]))
        later = lax.broadcasted_iota(jnp.int32, (1, 2 * c2), 1) >= c2
        for q in range(9):
            depth = min(5 * c1, width - 128 * q)
            keep = jnp.where(later, half_inside(4 * q + 2 - 14), half_inside(4 * q - 14)).astype(BF16)
            h1[:, 128 * q : 128 * (q + 1)] = gelu(dot(h0[:, 128 * q : 128 * q + depth], one_wide[:depth, :]), keep)
        for n in range(8):
            h2[:, 128 * n : 128 * (n + 1)] = gelu(
                dot(h1[:, 128 * n : 128 * n + 192], two[...]), flat_half(4 * n - 12, 128)
            )
        for k in range(2):
            for p in range(3):
                at = 256 * p + 128 * k
                h3[k * ROWS : (k + 1) * ROWS, 256 * p : 256 * (p + 1)] = gelu(
                    dot(h2[:, at : at + 384], three[...]), flat_half(APART * k + 8 * p - 8, 256)
                )
        rows = pl.ds(pl.multiple_of(block * ROWS, ROWS), ROWS)
        own_rows = pl.ds(pl.multiple_of(step * ROWS, ROWS), ROWS)
        parts = [slice(k * ROWS, (k + 1) * ROWS) for k in range(2)]
        features = [gelu(dot(h3[part, :], four[...])) for part in parts]
        tails = [dot(f, embed[...]).astype(BF16) for f in features]
        for k in range(2):
            normed = normalize(tails[k], gain_one[...])
            for q in range(model // 256):
                cols = slice(q * 256, (q + 1) * 256)
                keys[k, rows, cols] = dot(normed, pin[:, model + q * 256 : model + (q + 1) * 256]).astype(BF16)
                values[k, rows, cols] = dot(normed, pin[:, 2 * model + q * 256 : 2 * model + (q + 1) * 256]).astype(BF16)
            if mine:
                embedded[k, own_rows, :] = tails[k]
                for q in range(model // 256):
                    cols = slice(q * 256, (q + 1) * 256)
                    queries[k, own_rows, cols] = (dot(normed, pin[:, cols]).astype(BF16).astype(jnp.float32) * (head**-0.5)).astype(BF16)

    looped(half_blocks, functools.partial(convolve, True))
    looped(half_blocks, functools.partial(convolve, False))

    for load in loads[11:]:
        load.wait()

    def back(k, place):
        return pltpu.make_async_remote_copy(
            src_ref=result.at[k, place],
            dst_ref=out.at[slot_of(my_place) + APART * k],
            send_sem=out_send.at[k, place],
            recv_sem=out_recv.at[slot_of(my_place) + APART * k],
            device_id=(my_t, my_half * mates + place),
            device_id_type=MESH,
        )

    def keep_own(k):
        return pltpu.make_async_copy(
            result.at[k, my_place], out.at[slot_of(my_place) + APART * k], own_sem.at[k]
        )

    def encode(k, step):
        rows = pl.ds(pl.multiple_of(step * ROWS, ROWS), ROWS)
        first_head = lax.broadcasted_iota(jnp.int32, (1, 2 * head), 1) < head
        unit = (lax.broadcasted_iota(jnp.int32, (2 * ROWS, 128), 1) == 0).astype(jnp.float32).astype(BF16)
        ones = jnp.ones((tokens, 128), BF16)
        nothing = jnp.zeros((ROWS, 2 * head), BF16)
        def score(base):
            cols = slice(base, base + 2 * head)
            pair = queries[k, rows, cols]
            stacked = jnp.concatenate(
                [jnp.where(first_head, pair, nothing), jnp.where(first_head, nothing, pair)], axis=0
            )
            return dot_nt(
                jnp.concatenate([stacked, unit], axis=1), jnp.concatenate([keys[k, :, cols], key_bias[...]], axis=1)
            )

        def save(i, scores):
            cols = slice(2 * head * i, 2 * head * (i + 1))
            exponent = jnp.exp((scores - jnp.max(scores, axis=1, keepdims=True)).astype(BF16))
            mean = dot(exponent, jnp.concatenate([values[k, :, cols], ones], axis=1))
            summed = jnp.where(first_head, mean[:ROWS, :128], mean[ROWS:, :128])
            total = jnp.where(first_head, mean[:ROWS, 128:], mean[ROWS:, 128:])
            attended[:, cols] = (summed / total).astype(BF16)

        staged(model // (2 * head), lambda i: score(2 * head * i), save, 4)
        mixed = (embedded[k, rows, :].astype(jnp.float32) + dot(attended[...], pout[...])).astype(BF16)
        normed = normalize(mixed, gain_two[...])
        def save_inner(q, part):
            inner[:, 256 * q : 256 * (q + 1)] = gelu(part)

        staged(up.shape[1] // 256, lambda q: dot(normed, up[:, 256 * q : 256 * (q + 1)]), save_inner)
        total = mixed.astype(jnp.float32) + dot(inner[...], down[...])
        result[k, pl.ds(step * chans, chans)] = total.astype(BF16).reshape(chans, held, model)

    for k in range(2):
        looped(half_blocks, functools.partial(encode, k))
        looped(mates - 1, lambda i: back(k, lax.rem(my_place + 1 + i, mates)).start())
        keep_own(k).start()

    looped(groups_t - 1, lambda i: hand(time_peer(i), my_t).wait_send())
    looped(groups_c - 1, lambda i: spread(chan_peer(i), my_c).wait_send())

    for k in range(2):

        def finish(i):
            place = lax.rem(my_place + 1 + i, mates)
            back(k, place).wait_send()
            at = slot_of(place) + APART * k
            pltpu.make_async_remote_copy(
                src_ref=result.at[k, place],
                dst_ref=out.at[at],
                send_sem=out_send.at[k, place],
                recv_sem=out_recv.at[at],
                device_id=(my_t, my_half * mates + place),
                device_id_type=MESH,
            ).wait_recv()

        looped(mates - 1, finish)
        keep_own(k).wait()


def per_device(
    samples,
    dead_channels,
    first_kernel,
    dilated_one,
    dilated_two,
    dilated_three,
    dilated_four,
    embed_weight,
    gain_one,
    project_in,
    project_out,
    gain_two,
    up_weight,
    down_weight,
):
    groups_t, groups_c = lax.axis_size("tm"), lax.axis_size("chan")
    held, slab = samples.shape
    assert slab // STRIDE == groups_c and groups_c % (2 * APART) == 0 and (groups_c // 2 * held) % ROWS == 0
    tokens = groups_c * held
    mates = groups_c // 2
    model = embed_weight.shape[1]
    flat = [w.reshape(w.shape[0] * w.shape[1], w.shape[2]) for w in (dilated_one, dilated_two, dilated_three, dilated_four)]
    width = SPAN * first_kernel.shape[1]
    anywhere = pl.BlockSpec(memory_space=pl.ANY)
    like = lambda w: pltpu.VMEM(w.shape, w.dtype)
    vmem = lambda *shape: pltpu.VMEM(shape, BF16)
    dma = pltpu.SemaphoreType.DMA
    return pl.pallas_call(
        functools.partial(kernel, groups_t, groups_c),
        out_shape=pltpu.VMEM((groups_c, held, model), BF16),
        in_specs=[anywhere] * 14,
        out_specs=anywhere,
        scratch_shapes=[
            vmem(groups_t, slab, held),
            vmem(groups_c, held, groups_t * slab),
            vmem(groups_t * slab, width),
            vmem(5 * dilated_one.shape[1], 2 * dilated_one.shape[2]),
            vmem(tokens, 128),
            vmem(ROWS, width),
            vmem(ROWS, 9 * 128),
            vmem(ROWS, 8 * 128),
            vmem(2 * ROWS, 3 * 256),
            vmem(2, tokens // 2, model),
            vmem(2, tokens // 2, model),
            vmem(2, tokens, model),
            vmem(2, tokens, model),
            vmem(ROWS, model),
            vmem(ROWS, up_weight.shape[1]),
            vmem(2, mates, held, model),
            pltpu.SMEM(dead_channels.shape, dead_channels.dtype),
            like(first_kernel),
            like(flat[0]),
            pltpu.VMEM((1, model), jnp.float32),
            pltpu.VMEM((1, model), jnp.float32),
        ]
        + [like(w) for w in flat[1:]]
        + [like(w) for w in (embed_weight, project_in, project_out, up_weight, down_weight)]
        + [
            dma((14,)),
            dma((groups_c,)),
            dma((groups_c,)),
            dma((groups_t,)),
            dma((groups_t,)),
            dma((2, mates)),
            dma((groups_c,)),
            dma((2,)),
            pltpu.SemaphoreType.REGULAR,
        ],
        compiler_params=pltpu.CompilerParams(
            collective_id=0, has_side_effects=True, vmem_limit_bytes=44 * 2**20
        ),
    )(
        *[
            pltpu.with_memory_space_constraint(w, pltpu.HBM)
            for w in (
                dead_channels,
                samples.T,
                first_kernel,
                *flat,
                embed_weight,
                gain_one.reshape(1, -1),
                project_in,
                project_out,
                gain_two.reshape(1, -1),
                up_weight,
                down_weight,
            )
        ]
    )


def solution(mesh):
    return jax.shard_map(
        per_device,
        mesh=mesh,
        in_specs=(P("chan", "tm"), P(), P(), P(), P(), P(), P(), P(), P(), P(), P(), P(), P(), P()),
        out_specs=P("tm", "chan", None),
        check_vma=False,
    )
```
